32 devices in a mesh: depth: 4 (over z), width: 2 (over x), hidden: 4 (over y, core).
Axes of the slice: x: 2, y: 2, z: 4, core: 2. Of those that a mesh axis runs over, the one named last changes fastest.
Arguments:
- inputs: float32 [4096, 3072], P('depth', 'width'), may hold values from -6 to 6
- weight: float32 [3072, 12288], P('width', ('hidden', 'depth')), may hold values from -0.15625 to 0.15625
- cotangent: float32 [4096, 12288], P('depth', 'hidden'), may hold values from -6 to 6
Outputs:
- input_grad: float32 [4096, 3072], P('depth', ('width', 'hidden'))
- weight_grad: float32 [3072, 12288], P('width', ('hidden', 'depth'))
The draws below stay inside these ranges and needn't reach their ends.
All inputs are finite; a program needn't handle non-finite values.
Results may differ from the reference program's by a relative error of at most 0.00011.
Values sent between devices are 32-bit elements; how exact they have to be, the bound alone decides.
No kernel may reach another device: no remote copies, remote signals or barrier semaphores. Data moves between devices by JAX's collectives and lax.ppermute only.
A program may use at most 192 MiB of HBM per device.

```python
import jax
import jax.numpy as jnp
from jax import lax

D = 3072
F = 12288
TOKENS = 4096


def strengthened(entries, key, source, target, parts, factor):
    def block_of(position):
        return (jnp.arange(entries.shape[position]) // (entries.shape[position] // parts)).reshape((-1,) + (1,) * (entries.ndim - 1 - position))

    near = jax.random.permutation(key, parts)[block_of(target)]
    other_side = (block_of(target) + parts // 2) % parts
    return jnp.where((block_of(source) == near) | (block_of(source) == other_side), factor * entries, entries)


def level_of(rng, extent, shards, smallest, largest):
    def one(dim, shards_of):
        steps = jax.random.uniform(jax.random.fold_in(jax.random.fold_in(rng, 6), dim), (shards_of,), jnp.float32, smallest / len(shards), largest / len(shards))
        return jnp.repeat(jnp.exp(steps), extent[dim] // shards_of).reshape((-1,) + (1,) * (len(extent) - dim - 1))

    factor_of = one(*shards[0])
    for cut in shards[1:]:
        factor_of = factor_of * one(*cut)
    return factor_of


def scatter_about(stream_key, extent, scale, reach, split=(), kind=jnp.bfloat16):
    loudness = level_of(stream_key, extent, split, -0.22, 0.18) if split else 1.0
    entries = jax.random.normal(stream_key, extent, jnp.float32) * scale * loudness
    return jnp.minimum(jnp.maximum(entries, -reach), reach).astype(kind)


def noise_with(key, extent, deviation, bound, split, heavy, dtype=jnp.bfloat16):
    result = deviation * jax.random.normal(key, extent, jnp.float32)
    if split:
        result = result * level_of(key, extent, split, -0.22, 0.18)
    return jnp.clip(strengthened(result, jax.random.fold_in(key, 3), *heavy), -bound, bound).astype(dtype)


def setup_inputs(seed: int = 0) -> dict:
    streams_of = jax.random.split(jax.random.key(seed), 4)
    return {
        "inputs": scatter_about(streams_of[0], (TOKENS, D), 1.0, 6.0, ((0, 4), (1, 2)), jnp.float32),
        "weight": noise_with(streams_of[1], (D, F), D ** -0.5, 0.15625, ((0, 2), (1, 16)), (1, 0, 16, 2.0), jnp.float32),
        "cotangent": noise_with(streams_of[2], (TOKENS, F), 1.0, 6.0, ((0, 4), (1, 4)), (0, 1, 4, 2.0), jnp.float32),
    }


inv_sqrt_two = 0.7071067811865476
inv_sqrt_two_pi = 0.3989422804014327

def gelu_slope(preact):
    cumulative = 0.5 * (1.0 + jax.scipy.special.erf(preact * inv_sqrt_two))
    density = jnp.exp(-0.5 * preact * preact) * inv_sqrt_two_pi
    return cumulative + preact * density

def reference(inputs, weight, cotangent):
    preact = jnp.dot(inputs, weight, precision=lax.Precision.HIGHEST, preferred_element_type=jnp.float32)
    pre_grad = cotangent * gelu_slope(preact)
    input_grad = jnp.dot(pre_grad, weight.T, precision=lax.Precision.HIGHEST, preferred_element_type=jnp.float32)
    weight_grad = jnp.dot(inputs.T, pre_grad, precision=lax.Precision.HIGHEST, preferred_element_type=jnp.float32)
    return (input_grad, weight_grad)
```

```python
import jax
import jax.numpy as jnp
from jax import lax
from jax.sharding import PartitionSpec as P


inv_sqrt_two = 0.7071067811865476
inv_sqrt_two_pi = 0.3989422804014327

PARTS = (4, 7, 5)


def gelu_slope(preact):
    cumulative = 0.5 * (1.0 + jax.scipy.special.erf(preact * inv_sqrt_two))
    density = jnp.exp(-0.5 * preact * preact) * inv_sqrt_two_pi
    return cumulative + preact * density


def product(left, right, dims):
    return lax.dot_general(
        left,
        right,
        (dims, ((), ())),
        precision=lax.Precision.HIGH,
        preferred_element_type=jnp.float32,
    )


def make_local(mesh):
    depth, width, hidden = (mesh.shape[name] for name in ("depth", "width", "hidden"))
    pairs = hidden // 2

    def width_shift(values, by):
        return lax.ppermute(values, "width", [(i, (i + by) % width) for i in range(width)])

    def depth_shift(values, by):
        return lax.ppermute(values, "depth", [(i, (i + by) % depth) for i in range(depth)])

    def twin_swap(values):
        return lax.ppermute(values, "hidden", [(i, i ^ 1) for i in range(hidden)])

    def pair_shift(values, by):
        return lax.ppermute(
            values, "hidden", [(i, ((i // 2 + by) % pairs) * 2 + i % 2) for i in range(hidden)]
        )

    def up(values, first, last):
        return lax.ppermute(values, "depth", [(i, i + 1) for i in range(first, last)])

    def down(values, first, last):
        return lax.ppermute(
            values, "depth", [(depth - 1 - i, depth - 2 - i) for i in range(first, last)]
        )

    def local(inputs, weight, cotangent):
        tokens, model = inputs.shape
        units = weight.shape[1]
        block = model // hidden
        half = tokens // width
        sizes = [half * part // sum(PARTS) for part in PARTS]
        starts = [sum(sizes[:p]) for p in range(len(sizes))]
        z = lax.axis_index("depth")
        x = lax.axis_index("width")
        h = lax.axis_index("hidden")
        y, c = h // 2, h % 2
        order = [
            ((y + k) % pairs) * 2 + core
            for core in (1 - c, c)
            for k in [*range(1, pairs), 0]
        ]
        sides = [(x + k) % width for k in [*range(1, width), 0]]
        twin_weight, near_weight = (
            jnp.concatenate([lax.dynamic_slice_in_dim(weight, b * block, block, 0) for b in part])
            for part in (order[:pairs], order[pairs:])
        )

        def after(values, *others):
            return lax.optimization_barrier((values, *others))[0]

        gathered = []
        per_side = hidden // width
        for p, rows in enumerate(sizes):
            share = rows // per_side
            first = (h // per_side) * half + starts[p] + (h % per_side) * share
            piece = lax.dynamic_slice_in_dim(inputs, first, share, 0)
            below, above = [piece], [piece]
            for s in range(1, depth):
                below.append(up(below[-1], s - 1, depth - 1))
                above.append(down(above[-1], s - 1, depth - 1))
            column = jnp.stack(
                [jnp.where(z >= k, below[k], above[depth - k]) for k in range(1, depth)]
            )
            gathered.append(
                lax.all_gather(column, "hidden", axis=0, tiled=False)
            )

        def cot_rows(first, extent, column):
            return lax.dynamic_slice(cotangent, (first, column * units), (extent, units))

        def far_rows(p):
            parts = []
            for k in range(1, depth):
                piece = cot_rows(x * half + starts[p], sizes[p], (z + k) % depth)
                parts.append(depth_shift(piece, k))
            return parts

        def partials(blocks):
            sent = [product(b, weight, ((1,), (0,))) for b in blocks[:-1]]
            moved = [width_shift(s, k + 1) for k, s in enumerate(sent)]
            kept = product(blocks[-1], weight, ((1,), (0,)))
            return [after(kept, *sent), *moved]

        def slope_of(partial, cot):
            preact = partial[0]
            for part in partial[1:]:
                preact = preact + part
            return cot * gelu_slope(preact)

        def over_hidden(grad):
            twin_part = product(grad, twin_weight, ((1,), (1,)))
            twin_part = twin_swap(twin_part)
            near = product(grad, near_weight, ((1,), (1,))) + twin_part
            total = near[:, (pairs - 1) * block :]
            for k in range(1, pairs):
                moved = pair_shift(near[:, (k - 1) * block : k * block], k)
                total = total + moved
            return total

        def over_depth(sums):
            placed = jnp.concatenate(
                [
                    lax.dynamic_index_in_dim(sums, (z - d) % depth, 0, False).reshape(-1, block)
                    for d in range(depth)
                ]
            )
            placed = after(placed, *finished)
            total = lax.psum_scatter(placed, "depth", scatter_dimension=0, tiled=True)
            finished[:] = [total]
            return total

        weight_sum, gate, finished = [], [], []

        def weight_part(block_rows, grad):
            term = product(block_rows, grad, ((0,), (0,)))
            total = weight_sum[0] + term if weight_sum else term
            weight_sum[:] = [after(total)]

        def group(blocks, cot):
            partial = partials(blocks)
            grad = slope_of(partial, cot)
            others = [width_shift(grad, -k) for k in range(1, width)]
            gate[:] = [grad]
            own_sum = over_hidden(grad)
            weight_part(blocks[-1], grad)
            sums = []
            for k, g in enumerate(others):
                sums.append(over_hidden(g))
                weight_part(blocks[k], g)
            return [*sums, own_sum]

        blocks = [lax.dynamic_slice_in_dim(inputs, s * half, half, 0) for s in sides]
        totals = group(blocks, cot_rows(x * half, half, z))

        arrived = []
        for p, rows in enumerate(sizes):
            share = rows // per_side
            cots = far_rows(p)
            here = after(gathered[p], *gate)
            blocks = [
                lax.dynamic_slice_in_dim(here, s * per_side, per_side, 0).reshape(-1, model)
                for s in sides
            ]
            cot = jnp.stack([c.reshape(per_side, share, units) for c in cots], axis=1)
            sums = [
                [s.reshape(per_side, depth - 1, share, block)[:, k] for k in range(depth - 1)]
                for s in group(blocks, cot.reshape(-1, units))
            ]
            parts = []
            for q, side in enumerate(sums):
                base = totals[q][starts[p] : starts[p] + rows].reshape(per_side, share, block)
                parts.append(jnp.stack([base, *side]))
            if p < len(sizes) - 1:
                arrived.append(over_depth(jnp.stack(parts, axis=1)).reshape(width, rows, block))
            else:
                own = over_depth(parts[-1]).reshape(1, rows, block)
                others = over_depth(jnp.stack(parts[:-1], axis=1))
                arrived.append(jnp.concatenate([others.reshape(-1, rows, block), own]))
        stacked = jnp.concatenate(arrived, axis=1)
        input_grad = jnp.concatenate(
            [
                lax.dynamic_index_in_dim(stacked, (a - x - 1) % width, 0, keepdims=False)
                for a in range(width)
            ]
        )
        return input_grad, weight_sum[0]

    return local


def solution(mesh):
    placed = (P("depth", "width"), P("width", ("hidden", "depth")), P("depth", "hidden"))
    local = make_local(mesh)

    return jax.shard_map(
        local,
        mesh=mesh,
        in_specs=placed,
        out_specs=(P("depth", ("width", "hidden")), P("width", ("hidden", "depth"))),
        check_vma=False,
    )
```

```python
import jax
import jax.numpy as jnp
from jax import lax
from jax.sharding import PartitionSpec as P


inv_sqrt_two = 0.7071067811865476
inv_sqrt_two_pi = 0.3989422804014327

PARTS = (4, 7, 5)


def gelu_slope(preact):
    cumulative = 0.5 * (1.0 + jax.scipy.special.erf(preact * inv_sqrt_two))
    density = jnp.exp(-0.5 * preact * preact) * inv_sqrt_two_pi
    return cumulative + preact * density


def product(left, right, dims):
    return lax.dot_general(
        left,
        right,
        (dims, ((), ())),
        precision=lax.Precision.HIGH,
        preferred_element_type=jnp.float32,
    )


def make_local(mesh):
    depth, width, hidden = (mesh.shape[name] for name in ("depth", "width", "hidden"))
    pairs = hidden // 2

    def width_shift(values, by):
        return lax.ppermute(values, "width", [(i, (i + by) % width) for i in range(width)])

    def depth_shift(values, by):
        return lax.ppermute(values, "depth", [(i, (i + by) % depth) for i in range(depth)])

    def twin_swap(values):
        return lax.ppermute(values, "hidden", [(i, i ^ 1) for i in range(hidden)])

    def pair_shift(values, by):
        return lax.ppermute(
            values, "hidden", [(i, ((i // 2 + by) % pairs) * 2 + i % 2) for i in range(hidden)]
        )

    def up(values, first, last):
        return lax.ppermute(values, "depth", [(i, i + 1) for i in range(first, last)])

    def down(values, first, last):
        return lax.ppermute(
            values, "depth", [(depth - 1 - i, depth - 2 - i) for i in range(first, last)]
        )

    def local(inputs, weight, cotangent):
        tokens, model = inputs.shape
        units = weight.shape[1]
        block = model // hidden
        half = tokens // width
        sizes = [half * part // sum(PARTS) for part in PARTS]
        starts = [sum(sizes[:p]) for p in range(len(sizes))]
        z = lax.axis_index("depth")
        x = lax.axis_index("width")
        h = lax.axis_index("hidden")
        y, c = h // 2, h % 2
        order = [
            ((y + k) % pairs) * 2 + core
            for core in (1 - c, c)
            for k in [*range(1, pairs), 0]
        ]
        sides = [(x + k) % width for k in [*range(1, width), 0]]
        twin_weight, near_weight = (
            jnp.concatenate([lax.dynamic_slice_in_dim(weight, b * block, block, 0) for b in part])
            for part in (order[:pairs], order[pairs:])
        )

        def after(values, *others):
            return lax.optimization_barrier((values, *others))[0]

        gathered = []
        per_side = hidden // width
        for p, rows in enumerate(sizes):
            share = rows // per_side
            first = (h // per_side) * half + starts[p] + (h % per_side) * share
            piece = lax.dynamic_slice_in_dim(inputs, first, share, 0)
            below, above = [piece], [piece]
            for s in range(1, depth):
                below.append(up(below[-1], s - 1, depth - 1))
                above.append(down(above[-1], s - 1, depth - 1))
            column = jnp.stack(
                [jnp.where(z >= k, below[k], above[depth - k]) for k in range(1, depth)]
            )
            gathered.append(
                lax.all_gather(column, "hidden", axis=0, tiled=False)
            )

        def cot_rows(first, extent, column):
            return lax.dynamic_slice(cotangent, (first, column * units), (extent, units))

        def far_rows(p):
            parts = []
            for k in range(1, depth):
                piece = cot_rows(x * half + starts[p], sizes[p], (z + k) % depth)
                parts.append(depth_shift(piece, k))
            return parts

        def partials(blocks):
            sent = [product(b, weight, ((1,), (0,))) for b in blocks[:-1]]
            moved = [width_shift(s, k + 1) for k, s in enumerate(sent)]
            kept = product(blocks[-1], weight, ((1,), (0,)))
            return [after(kept, *sent), *moved]

        def slope_of(partial, cot):
            preact = partial[0]
            for part in partial[1:]:
                preact = preact + part
            return cot * gelu_slope(preact)

        def over_hidden(grad):
            twin_part = product(grad, twin_weight, ((1,), (1,)))
            twin_part = twin_swap(twin_part)
            near = product(grad, near_weight, ((1,), (1,))) + twin_part
            total = near[:, (pairs - 1) * block :]
            for k in range(1, pairs):
                moved = pair_shift(near[:, (k - 1) * block : k * block], k)
                total = total + moved
            return total

        def over_depth(sums):
            placed = jnp.concatenate(
                [
                    lax.dynamic_index_in_dim(sums, (z - d) % depth, 0, False).reshape(-1, block)
                    for d in range(depth)
                ]
            )
            placed = after(placed, *finished)
            total = lax.psum_scatter(placed, "depth", scatter_dimension=0, tiled=True)
            finished[:] = [total]
            return total

        weight_sum, gate, finished = [], [], []

        def weight_part(block_rows, grad):
            term = product(block_rows, grad, ((0,), (0,)))
            total = weight_sum[0] + term if weight_sum else term
            weight_sum[:] = [after(total)]

        def group(blocks, cot):
            partial = partials(blocks)
            grad = slope_of(partial, cot)
            others = [width_shift(grad, -k) for k in range(1, width)]
            gate[:] = [grad]
            own_sum = over_hidden(grad)
            weight_part(blocks[-1], grad)
            sums = []
            for k, g in enumerate(others):
                sums.append(over_hidden(g))
                weight_part(blocks[k], g)
            return [*sums, own_sum]

        blocks = [lax.dynamic_slice_in_dim(inputs, s * half, half, 0) for s in sides]
        totals = group(blocks, cot_rows(x * half, half, z))

        arrived = []
        for p, rows in enumerate(sizes):
            share = rows // per_side
            cots = far_rows(p)
            here = after(gathered[p], *gate)
            blocks = [
                lax.dynamic_slice_in_dim(here, s * per_side, per_side, 0).reshape(-1, model)
                for s in sides
            ]
            cot = jnp.stack([c.reshape(per_side, share, units) for c in cots], axis=1)
            sums = [
                [s.reshape(per_side, depth - 1, share, block)[:, k] for k in range(depth - 1)]
                for s in group(blocks, cot.reshape(-1, units))
            ]
            parts = []
            for side in sums:
                parts.append(jnp.stack([jnp.zeros_like(side[0]), *side]))
            arrived.append(over_depth(jnp.stack(parts, axis=1)).reshape(width, rows, block))
        stacked = jnp.concatenate(arrived, axis=1) + jnp.stack(totals)
        input_grad = jnp.concatenate(
            [
                lax.dynamic_index_in_dim(stacked, (a - x - 1) % width, 0, keepdims=False)
                for a in range(width)
            ]
        )
        return input_grad, weight_sum[0]

    return local


def solution(mesh):
    placed = (P("depth", "width"), P("width", ("hidden", "depth")), P("depth", "hidden"))
    local = make_local(mesh)

    return jax.shard_map(
        local,
        mesh=mesh,
        in_specs=placed,
        out_specs=(P("depth", ("width", "hidden")), P("width", ("hidden", "depth"))),
        check_vma=False,
    )
```
